512 devices in a mesh: bead: 32 (over y_lo, z, core), slab: 16 (over y_hi, x).
Axes of the slice: x: 4, y: 8 (y_hi: 4, y_lo: 2; y = y_hi * 2 + y_lo), z: 8, core: 2. Of those that a mesh axis runs over, the one named last changes fastest.
Arguments:
- positions: float32 [32, 3, 16, 4, 4, 128], P('bead', None, 'slab'), may hold values from 0 to 1
- velocities: float32 [32, 3, 16, 4, 4, 128], P('bead', None, 'slab'), may hold values from -6 to 6
- counts: int32 [16, 4, 4], P('slab'), may hold values from 64 to 128
Outputs:
- positions_out: float32 [32, 3, 16, 4, 4, 128], P('bead', None, 'slab')
- velocities_out: float32 [32, 3, 16, 4, 4, 128], P('bead', None, 'slab')
The draws below stay inside these ranges and needn't reach their ends.
Inputs may be any that keep to these rules, and one draw needn't show every extreme that they name: `counts`: a cell's atoms occupy its slots 0 to count - 1; the other slots are empty.
All inputs are finite; a program needn't handle non-finite values.
Results may differ from the reference program's by a relative error of at most 0.0001.
Values sent between devices are 32-bit elements; how exact they have to be, the bound alone decides.
A program may use at most 64 MiB of HBM per device.

```python
import jax
import jax.numpy as jnp
from jax import lax

S = 128
GY = 4
GZ = 4
STEPS = 4
BEADS = 32
NX = 16


def set_ends(entries, rng, low, largest):
    spot = [jax.random.randint(jax.random.fold_in(rng, axis), (), 0, length) for axis, length in enumerate(entries.shape)]
    main_axis = entries.shape.index(max(entries.shape))
    neighbour = spot[:main_axis] + [(spot[main_axis] + 1) % entries.shape[main_axis]] + spot[main_axis + 1:]
    return entries.at[tuple(spot)].set(low).at[tuple(neighbour)].set(largest)


def levels(own_key, dims, split, least, largest):
    level, own = 1.0, jax.random.fold_in(own_key, 6)
    for position, parts in split:
        steps = jnp.exp(jax.random.uniform(jax.random.fold_in(own, position), (parts,), jnp.float32, least / len(split), largest / len(split)))
        level = level * jnp.repeat(steps, dims[position] // parts).reshape([-1 if axis == position else 1 for axis in range(len(dims))])
    return level


def gaussian(stream_key, extent, spread, bound, shards=(), held_as=jnp.bfloat16):
    factor_of = levels(stream_key, extent, shards, -0.22, 0.18) if shards else 1.0
    array = jax.random.normal(stream_key, extent, jnp.float32) * spread * factor_of
    return jnp.minimum(jnp.maximum(array, -bound), bound).astype(held_as)


def setup_inputs(seed: int = 0) -> dict:
    streams_of = jax.random.split(jax.random.key(seed), 4)
    return {
        "positions": jnp.clip(1.0 * jax.random.uniform(streams_of[0], (BEADS, 3, NX, GY, GZ, S), jnp.float32) ** levels(streams_of[0], (BEADS, 3, NX, GY, GZ, S), ((0, 32), (2, 16)), -0.2, 0.2), 0.0, 1.0),
        "velocities": gaussian(streams_of[1], (BEADS, 3, NX, GY, GZ, S), 1.0, 6.0, ((0, 32), (2, 16)), jnp.float32),
        "counts": set_ends(jax.random.randint(streams_of[2], (NX, GY, GZ), S // 2, S + 1), jax.random.fold_in(streams_of[2], 1), S // 2, S).astype(jnp.int32),
    }


PAIR_SCALE = 0.08
WIDTH_FACTOR = 2.0
SPRING = 4.0
HALF_STEP = 0.025
TIME_STEP = 0.05


def cell_offsets():
    listing = []
    for along_x in (-1, 0, 1):
        for along_y in (-1, 0, 1):
            for along_z in (-1, 0, 1):
                listing.append((along_x, along_y, along_z))
    return listing


def pair_term(own_parts, near_parts, near_mask, offset):
    deltas = []
    for component in range(3):
        deltas.append(own_parts[component][..., :, None] - near_parts[component][..., None, :] - float(offset[component]))
    squared = deltas[0] * deltas[0] + deltas[1] * deltas[1] + deltas[2] * deltas[2]
    weights = PAIR_SCALE * jnp.exp(-WIDTH_FACTOR * squared) * near_mask[..., None, :]
    return weights, deltas


def bead_pair_force(coords, present):
    own_parts = [coords[0], coords[1], coords[2]]
    summed = [jnp.zeros_like(coords[0]) for component in range(3)]
    for offset in cell_offsets():
        rolled = jnp.roll(coords, (-offset[0], -offset[1], -offset[2]), axis=(1, 2, 3))
        rolled_mask = jnp.roll(present, (-offset[0], -offset[1], -offset[2]), axis=(0, 1, 2))
        weights, deltas = pair_term(own_parts, [rolled[0], rolled[1], rolled[2]], rolled_mask, offset)
        for component in range(3):
            summed[component] = summed[component] + jnp.sum(weights * deltas[component], axis=-1)
    return jnp.stack(summed) * present


def reference(positions, velocities, counts):
    slot_ids = lax.broadcasted_iota(jnp.int32, counts.shape + (positions.shape[-1],), 3)
    present = (slot_ids < counts[..., None]).astype(jnp.float32)

    def total_forces(coords):
        paired = lax.map(lambda single_bead: bead_pair_force(single_bead, present), coords)
        before = jnp.roll(coords, 1, axis=0)
        behind = jnp.roll(coords, -1, axis=0)
        spring = -SPRING * ((2.0 * coords - before) - behind)
        return paired + spring

    forces = total_forces(positions)
    for step_index in range(STEPS):
        velocities = velocities + HALF_STEP * forces
        positions = positions + TIME_STEP * velocities
        forces = total_forces(positions)
        velocities = velocities + HALF_STEP * forces
    return positions, velocities
```

```python
import functools

import jax
import jax.numpy as jnp
from jax import lax
from jax.experimental import pallas as pl
from jax.experimental.pallas import tpu as pltpu
from jax.sharding import PartitionSpec as P

STEPS = 4
EVALS = STEPS + 1

PAIR_SCALE = 0.08
WIDTH_FACTOR = 2.0
SPRING = 4.0
HALF_STEP = 0.025
TIME_STEP = 0.05

LOG2E = 1.4426950408889634
ALPHA = WIDTH_FACTOR * LOG2E
ABSENT = -1e30

CELLS = 16
SLOTS = 128
FEATS = 32
MESH = pl.DeviceIdType.MESH


def split3(value):
    high = value.astype(jnp.bfloat16).astype(jnp.float32)
    rest = value - high
    mid = rest.astype(jnp.bfloat16).astype(jnp.float32)
    return high, mid, rest - mid


def far_rows(coords):
    rows = []
    for coord in coords:
        h, m, l = split3(coord)
        rows += [h, m, l, h, m, h]
    norm = -ALPHA * (coords[0] * coords[0] + coords[1] * coords[1] + coords[2] * coords[2])
    return rows + list(split3(norm))


def own_rows(coords):
    rows = []
    for coord in coords:
        h, m, l = split3((2.0 * ALPHA) * coord)
        rows += [h, h, h, m, m, l]
    norm = -ALPHA * (coords[0] * coords[0] + coords[1] * coords[1] + coords[2] * coords[2])
    return rows, list(split3(norm))


def kernel(
    beads, slabs,
    pos_in, vel_in, counts, pos_out, vel_out,
    qs, halo, chain, mask_own, mask_halo, ext, own32, far32, own_feats, far_feats,
    bcast, acc, sums, eye, pick,
    send_sem, recv_sem, mask_send, mask_recv, load_sem,
):
    bead, slab = lax.axis_index("bead"), lax.axis_index("slab")
    slab_up, slab_down = lax.rem(slab + 1, slabs), lax.rem(slab + slabs - 1, slabs)
    bead_up, bead_down = lax.rem(bead + 1, beads), lax.rem(bead + beads - 1, beads)
    partners = [(bead, slab_up), (bead, slab_down), (bead_up, slab), (bead_down, slab)]

    barrier = pltpu.get_barrier_semaphore()
    for partner in partners:
        pl.semaphore_signal(barrier, inc=1, device_id=partner, device_id_type=MESH)

    lanes = lax.broadcasted_iota(jnp.int32, (1, SLOTS), 1)
    for cell in range(CELLS):
        here = lanes < counts[0, cell // 4, cell % 4]
        mask_own[cell : cell + 1, :] = jnp.where(here, 0.0, ABSENT)
    qs[0] = pos_in[...]
    vel_out[...] = vel_in[...]

    one = jnp.ones((8, SLOTS), jnp.float32)
    zero = jnp.zeros((8, SLOTS), jnp.float32)
    for group in range(6):
        for row in (18, 19, 20, 24):
            own32[pl.ds(group * 8 * FEATS + row, 8, stride=FEATS), :] = one
        for row in range(25, FEATS):
            own32[pl.ds(group * 8 * FEATS + row, 8, stride=FEATS), :] = zero
    for group in range(6):
        for row in (21, 22, 23):
            far32[pl.ds(group * 8 * FEATS + row, 8, stride=FEATS), :] = one
        for row in range(25, FEATS):
            far32[pl.ds(group * 8 * FEATS + row, 8, stride=FEATS), :] = zero
    ext[...] = jnp.zeros_like(ext)
    row_id = lax.broadcasted_iota(jnp.int32, (SLOTS, SLOTS), 0)
    lane_id = lax.broadcasted_iota(jnp.int32, (SLOTS, SLOTS), 1)
    eye[...] = jnp.where(row_id == lane_id, 1.0, 0.0).astype(jnp.bfloat16)
    feat_id = lax.broadcasted_iota(jnp.int32, (FEATS, SLOTS), 0)
    for comp in range(3):
        first = 6 * comp
        chosen = (feat_id >= first) & (feat_id < first + 3)
        pick[:, comp * SLOTS : (comp + 1) * SLOTS] = jnp.where(chosen, 1.0, 0.0).astype(jnp.bfloat16)

    pl.semaphore_wait(barrier, 4)

    def mask_copy(side):
        return pltpu.make_async_remote_copy(
            src_ref=mask_own,
            dst_ref=mask_halo.at[1 - side],
            send_sem=mask_send.at[side],
            recv_sem=mask_recv.at[1 - side],
            device_id=partners[side],
            device_id_type=MESH,
        )

    def slab_copy(turn, side):
        return pltpu.make_async_remote_copy(
            src_ref=qs.at[turn],
            dst_ref=halo.at[turn, 1 - side],
            send_sem=send_sem.at[turn, side],
            recv_sem=recv_sem.at[turn, 1 - side],
            device_id=partners[side],
            device_id_type=MESH,
        )

    def bead_copy(turn, side):
        return pltpu.make_async_remote_copy(
            src_ref=qs.at[turn],
            dst_ref=chain.at[turn, 1 - side],
            send_sem=send_sem.at[turn, 2 + side],
            recv_sem=recv_sem.at[turn, 3 - side],
            device_id=partners[2 + side],
            device_id_type=MESH,
        )

    for side in range(2):
        mask_copy(side).start()

    cell_id = lax.broadcasted_iota(jnp.int32, (CELLS, SLOTS), 0)
    off_y = (cell_id // 4).astype(jnp.float32) - 2.0
    off_z = (cell_id % 4).astype(jnp.float32) - 2.0

    def put_far(layer, coords, masks):
        for half in range(2):
            sel = slice(8 * half, 8 * half + 8)
            rows = far_rows([coord[sel] for coord in coords])
            base = (layer * CELLS + 8 * half) * FEATS
            for k, row in enumerate(rows):
                far32[pl.ds(base + k, 8, stride=FEATS), :] = row
            far32[pl.ds(base + 24, 8, stride=FEATS), :] = masks[sel]
        for cell in range(CELLS):
            at = layer * CELLS + cell
            block = far32[at * FEATS : (at + 1) * FEATS, :].astype(jnp.bfloat16)
            turned = lax.dot_general(
                eye[...], block, (((1,), (1,)), ((), ())), preferred_element_type=jnp.float32
            )
            far_feats[at] = turned.astype(jnp.bfloat16)

    def put_own(q):
        for comp in range(3):
            for yy in range(6):
                y = (yy + 3) % 4
                first = comp * CELLS + 4 * y
                ext[comp, yy, 1:5, :] = q[first : first + 4]
                ext[comp, yy, 0:1, :] = q[first + 3 : first + 4]
                ext[comp, yy, 5:6, :] = q[first : first + 1]
        zz_off = lax.broadcasted_iota(jnp.int32, (8, SLOTS), 0).astype(jnp.float32) - 3.0
        for yy in range(6):
            coords = [ext[0, yy] - 0.5, ext[1, yy] + (yy - 3.0), ext[2, yy] + zz_off]
            rows, norm = own_rows(coords)
            base = yy * 8 * FEATS
            for k, row in enumerate(rows):
                own32[pl.ds(base + k, 8, stride=FEATS), :] = row
            for k, row in enumerate(norm):
                own32[pl.ds(base + 21 + k, 8, stride=FEATS), :] = row
        for yy in range(6):
            for zz in range(6):
                at = (yy * 8 + zz) * FEATS
                own_feats[yy, :, zz * SLOTS : (zz + 1) * SLOTS] = own32[at : at + FEATS, :].astype(
                    jnp.bfloat16
                )

    def pairs(group):
        ny = lax.rem(group, 4)
        for nz in range(4):
            feats = far_feats[group * 4 + nz]
            bcast[nz] = jnp.dot(feats, pick[...], preferred_element_type=jnp.float32)
            for dy in range(3):
                yy = ny + dy
                expo = jnp.dot(
                    feats,
                    own_feats[yy, :, nz * SLOTS : (nz + 3) * SLOTS],
                    preferred_element_type=jnp.float32,
                )
                parts = [[None] * 4 for _ in range(3)]
                for chunk in range(SLOTS // 8):
                    sel = slice(8 * chunk, 8 * chunk + 8)
                    far = [bcast[nz, sel, k * SLOTS : (k + 1) * SLOTS] for k in range(3)]
                    for dz in range(3):
                        w = jnp.exp2(expo[sel, dz * SLOTS : (dz + 1) * SLOTS])
                        terms = [w, w * far[0], w * far[1], w * far[2]]
                        for k in range(4):
                            old = parts[dz][k]
                            parts[dz][k] = terms[k] if old is None else old + terms[k]
                for dz in range(3):
                    for k in range(4):
                        acc[yy, nz + dz, k] += parts[dz][k]

    def turn_body(turn, carry):
        for side in range(2):
            slab_copy(turn, side).start()
            bead_copy(turn, side).start()
        q = qs[turn]
        x, y, z = q[0:16] - 0.5, q[16:32] + off_y, q[32:48] + off_z
        acc[...] = jnp.zeros_like(acc)
        put_own(q)
        put_far(0, [x, y, z], mask_own[...])

        @pl.loop(0, 4)
        def _(group):
            pairs(group)

        @pl.when(turn == 0)
        def _():
            for side in range(2):
                mask_copy(side).wait()

        for side in range(2):
            slab_copy(turn, side).wait()
        for side in range(2):
            near = halo[turn, side]
            shift = 0.5 if side == 0 else -1.5
            put_far(
                1 + side,
                [near[0:16] + shift, near[16:32] + off_y, near[32:48] + off_z],
                mask_halo[side],
            )

        @pl.loop(4, 12)
        def _(group):
            pairs(group)

        for cell in range(CELLS):
            cy, cz = cell // 4, cell % 4
            ys = [(cy + 1, 0.0)] + ([(5, 4.0)] if cy == 0 else []) + ([(0, -4.0)] if cy == 3 else [])
            zs = [(cz + 1, 0.0)] + ([(5, 4.0)] if cz == 0 else []) + ([(0, -4.0)] if cz == 3 else [])
            total = [None] * 4
            for yy, sy in ys:
                for zz, sz in zs:
                    got = [acc[yy, zz, k] for k in range(4)]
                    if sy:
                        got[2] = got[2] - sy * got[0]
                    if sz:
                        got[3] = got[3] - sz * got[0]
                    total = [g if t is None else t + g for t, g in zip(total, got)]
            for k in range(4):
                sums[k, cell : cell + 1, :] = jnp.sum(total[k], axis=0, keepdims=True)

        for side in range(2):
            bead_copy(turn, side).wait()
        before, behind = chain[turn, 1], chain[turn, 0]
        spring = -SPRING * ((2.0 * q - before) - behind)
        here = jnp.where(mask_own[...] == 0.0, PAIR_SCALE, 0.0)
        force = [
            (coord * sums[0] - sums[1 + k]) * here + spring[16 * k : 16 * k + 16]
            for k, coord in enumerate([x, y, z])
        ]
        finish = jnp.where(turn > 0, HALF_STEP, 0.0)
        begin = jnp.where(turn < STEPS, HALF_STEP, 0.0)
        after = jnp.minimum(turn + 1, STEPS)
        for k in range(3):
            sel = slice(16 * k, 16 * k + 16)
            v = vel_out[sel] + finish * force[k]
            v = v + begin * force[k]
            vel_out[sel] = v

            @pl.when(turn < STEPS)
            def _():
                qs[after, sel] = q[sel] + TIME_STEP * v
        return carry

    lax.fori_loop(0, EVALS, turn_body, 0)
    pos_out[...] = qs[STEPS]


def local(positions, velocities, counts):
    rows = 3 * CELLS
    beads, slabs = lax.axis_size("bead"), lax.axis_size("slab")
    f32, bf16 = jnp.float32, jnp.bfloat16
    vmem = pl.BlockSpec(memory_space=pltpu.VMEM)
    out = pl.pallas_call(
        functools.partial(kernel, beads, slabs),
        out_shape=[jax.ShapeDtypeStruct((rows, SLOTS), f32)] * 2,
        in_specs=[vmem, vmem, pl.BlockSpec(memory_space=pltpu.SMEM)],
        out_specs=[vmem, vmem],
        scratch_shapes=[
            pltpu.VMEM((EVALS, rows, SLOTS), f32),
            pltpu.VMEM((EVALS, 2, rows, SLOTS), f32),
            pltpu.VMEM((EVALS, 2, rows, SLOTS), f32),
            pltpu.VMEM((CELLS, SLOTS), f32),
            pltpu.VMEM((2, CELLS, SLOTS), f32),
            pltpu.VMEM((3, 6, 8, SLOTS), f32),
            pltpu.VMEM((48 * FEATS, SLOTS), f32),
            pltpu.VMEM((48 * FEATS, SLOTS), f32),
            pltpu.VMEM((6, FEATS, 6 * SLOTS), bf16),
            pltpu.VMEM((48, SLOTS, FEATS), bf16),
            pltpu.VMEM((4, SLOTS, 3 * SLOTS), f32),
            pltpu.VMEM((6, 6, 4, 8, SLOTS), f32),
            pltpu.VMEM((4, CELLS, SLOTS), f32),
            pltpu.VMEM((SLOTS, SLOTS), bf16),
            pltpu.VMEM((FEATS, 3 * SLOTS), bf16),
            pltpu.SemaphoreType.DMA((EVALS, 4)),
            pltpu.SemaphoreType.DMA((EVALS, 4)),
            pltpu.SemaphoreType.DMA((2,)),
            pltpu.SemaphoreType.DMA((2,)),
            pltpu.SemaphoreType.DMA((2,)),
        ],
        compiler_params=pltpu.CompilerParams(collective_id=0, has_side_effects=True),
        name="verlet",
    )(positions.reshape(rows, SLOTS), velocities.reshape(rows, SLOTS), counts)
    return tuple(o.reshape(positions.shape) for o in out)


def solution(mesh):
    spec = P("bead", None, "slab", None, None, None)
    return jax.shard_map(
        local,
        mesh=mesh,
        in_specs=(spec, spec, P("slab", None, None)),
        out_specs=(spec, spec),
        check_vma=False,
    )
```

```python
import functools

import jax
import jax.numpy as jnp
from jax import lax
from jax.experimental import pallas as pl
from jax.experimental.pallas import tpu as pltpu
from jax.sharding import PartitionSpec as P

STEPS = 4
EVALS = STEPS + 1

PAIR_SCALE = 0.08
WIDTH_FACTOR = 2.0
SPRING = 4.0
HALF_STEP = 0.025
TIME_STEP = 0.05

LOG2E = 1.4426950408889634
ALPHA = WIDTH_FACTOR * LOG2E
ABSENT = -1e30

CELLS = 16
SLOTS = 128
FEATS = 32
OWN_STRIDE, FAR_STRIDE = 33, 25
UNROLL = 16
MESH = pl.DeviceIdType.MESH


def split3(value):
    high = value.astype(jnp.bfloat16).astype(jnp.float32)
    rest = value - high
    mid = rest.astype(jnp.bfloat16).astype(jnp.float32)
    return high, mid, rest - mid


def far_rows(coords):
    rows = []
    for coord in coords:
        h, m, l = split3(coord)
        rows += [h, m, l, h, m, h]
    norm = -ALPHA * (coords[0] * coords[0] + coords[1] * coords[1] + coords[2] * coords[2])
    return rows + list(split3(norm))


def own_rows(coords):
    rows = []
    for coord in coords:
        h, m, l = split3((2.0 * ALPHA) * coord)
        rows += [h, h, h, m, m, l]
    norm = -ALPHA * (coords[0] * coords[0] + coords[1] * coords[1] + coords[2] * coords[2])
    return list(enumerate(rows)) + list(enumerate(split3(norm), 21))


def kernel(
    beads, slabs,
    pos_in, vel_in, counts, pos_out, vel_out,
    qs, halo, chain, mask_own, mask_halo, ext, own32, far32, own_feats, far_feats, far_coords,
    acc, columns, sums, eye,
    send_sem, recv_sem, mask_send, mask_recv,
):
    bead, slab = lax.axis_index("bead"), lax.axis_index("slab")
    slab_up, slab_down = lax.rem(slab + 1, slabs), lax.rem(slab + slabs - 1, slabs)
    bead_up, bead_down = lax.rem(bead + 1, beads), lax.rem(bead + beads - 1, beads)
    partners = [(bead, slab_up), (bead, slab_down), (bead_up, slab), (bead_down, slab)]
    near = jnp.where(lax.rem(slab, 4) == 3, 1, 0)
    order = [near, 1 - near]

    barrier = pltpu.get_barrier_semaphore()
    for partner in partners:
        pl.semaphore_signal(barrier, inc=1, device_id=partner, device_id_type=MESH)

    lanes = lax.broadcasted_iota(jnp.int32, (1, SLOTS), 1)
    for cell in range(CELLS):
        here = lanes < counts[0, cell // 4, cell % 4]
        mask_own[cell : cell + 1, :] = jnp.where(here, 0.0, ABSENT)
    qs[0] = pos_in[...]
    vel_out[...] = vel_in[...]

    pl.semaphore_wait(barrier, 4)

    def mask_copy(side):
        return pltpu.make_async_remote_copy(
            src_ref=mask_own,
            dst_ref=mask_halo.at[1 - side],
            send_sem=mask_send.at[side],
            recv_sem=mask_recv.at[1 - side],
            device_id=partners[side],
            device_id_type=MESH,
        )

    def slab_copy(turn, side):
        return pltpu.make_async_remote_copy(
            src_ref=qs.at[turn],
            dst_ref=halo.at[turn, 1 - side],
            send_sem=send_sem.at[turn, side],
            recv_sem=recv_sem.at[turn, 1 - side],
            device_id=partners[side],
            device_id_type=MESH,
        )

    def slab_landing(turn, side):
        return pltpu.make_async_remote_copy(
            src_ref=qs.at[turn],
            dst_ref=halo.at[turn, side],
            send_sem=send_sem.at[turn, 0],
            recv_sem=recv_sem.at[turn, side],
            device_id=partners[0],
            device_id_type=MESH,
        )

    def bead_copy(turn, side):
        return pltpu.make_async_remote_copy(
            src_ref=qs.at[turn],
            dst_ref=chain.at[turn, 1 - side],
            send_sem=send_sem.at[turn, 2 + side],
            recv_sem=recv_sem.at[turn, 3 - side],
            device_id=partners[2 + side],
            device_id_type=MESH,
        )

    def send(turn):
        for side in range(2):
            slab_copy(turn, side).start()
        for side in range(2):
            bead_copy(turn, side).start()

    for side in range(2):
        mask_copy(side).start()
    send(0)

    one = jnp.ones((8, SLOTS), jnp.float32)
    zero = jnp.zeros((8, SLOTS), jnp.float32)
    for group in range(2):
        for row in range(FEATS):
            if row in (18, 19, 20) or row >= 24:
                at = pl.ds(group * 8 * OWN_STRIDE + row, 8, stride=OWN_STRIDE)
                own32[at, :] = one if row <= 24 else zero
    for group in range(18):
        for row in (21, 22, 23):
            far32[pl.ds(group * 8 * FAR_STRIDE + row, 8, stride=FAR_STRIDE), :] = one
    far32[3 * 48 * FAR_STRIDE :, :] = zero
    ext[...] = jnp.zeros_like(ext)
    columns[...] = jnp.zeros_like(columns)
    row_id = lax.broadcasted_iota(jnp.int32, (SLOTS, SLOTS), 0)
    lane_id = lax.broadcasted_iota(jnp.int32, (SLOTS, SLOTS), 1)
    eye[...] = jnp.where(row_id == lane_id, 1.0, 0.0).astype(jnp.bfloat16)

    cell_id = lax.broadcasted_iota(jnp.int32, (CELLS, SLOTS), 0)
    off_y = (cell_id // 4).astype(jnp.float32) - 2.0
    off_z = (cell_id % 4).astype(jnp.float32) - 2.0
    zz_off = lax.broadcasted_iota(jnp.int32, (8, SLOTS), 0).astype(jnp.float32) - 3.0
    lane8 = lax.broadcasted_iota(jnp.int32, (8, SLOTS), 1)

    def extend(comp, rows):
        for yy in range(6):
            y = (yy + 3) % 4
            ext[comp, yy, 1:5, :] = rows[4 * y : 4 * y + 4]
            ext[comp, yy, 0:1, :] = rows[4 * y + 3 : 4 * y + 4]
            ext[comp, yy, 5:6, :] = rows[4 * y : 4 * y + 1]

    def put_mask(slot, mask):
        extend(0, mask)
        for yy in range(6):
            far32[pl.ds((slot * 48 + yy * 8) * FAR_STRIDE + 24, 8, stride=FAR_STRIDE), :] = ext[0, yy]

    def put_far(slot, q, shift):
        for comp in range(3):
            extend(comp, q[16 * comp : 16 * comp + 16])
        for yy in range(6):
            coords = [ext[0, yy] + shift, ext[1, yy] + (yy - 3.0), ext[2, yy] + zz_off]
            for comp in range(3):
                far_coords[slot, comp, yy] = coords[comp]
            base = (slot * 48 + yy * 8) * FAR_STRIDE
            for k, row in enumerate(far_rows(coords)):
                far32[pl.ds(base + k, 8, stride=FAR_STRIDE), :] = row
        for yy in range(6):
            for zz in range(6):
                at = (slot * 48 + yy * 8 + zz) * FAR_STRIDE
                far_feats[slot, yy, :, zz * SLOTS : (zz + 1) * SLOTS] = far32[
                    at : at + FEATS, :
                ].astype(jnp.bfloat16)

    def put_own(coords):
        for half in range(2):
            sel = slice(8 * half, 8 * half + 8)
            for k, row in own_rows([coord[sel] for coord in coords]):
                own32[pl.ds(8 * half * OWN_STRIDE + k, 8, stride=OWN_STRIDE), :] = row
        for cell in range(CELLS):
            block = own32[cell * OWN_STRIDE : cell * OWN_STRIDE + FEATS, :].astype(jnp.bfloat16)
            turned = lax.dot_general(
                eye[...], block, (((1,), (1,)), ((), ())), preferred_element_type=jnp.float32
            )
            own_feats[cell] = turned.astype(jnp.bfloat16)

    def pairs(cell, blocks, first, last):
        cy, cz = cell // 4, lax.rem(cell, 4)
        feats = own_feats[cell]
        for start in range(0, len(blocks), 4):
            group = blocks[start : start + 4]
            opening, closing = first and start == 0, last and start + 4 >= len(blocks)
            expo, far = [], []
            for tile in range(0, len(group), 2):
                sides = [
                    far_feats[slot, cy + dy, :, pl.ds(pl.multiple_of((cz + dz) * SLOTS, SLOTS), SLOTS)]
                    for slot, dy, dz in group[tile : tile + 2]
                ]
                side = sides[0] if len(sides) == 1 else jnp.concatenate(sides, axis=1)
                both = jnp.dot(feats, side, preferred_element_type=jnp.float32)
                expo += [both[:, n * SLOTS : (n + 1) * SLOTS] for n in range(len(sides))]
            for slot, dy, dz in group:
                far.append(
                    [
                        jnp.broadcast_to(
                            far_coords[slot, k, cy + dy, pl.ds(cz + dz, 1), :], (8, SLOTS)
                        )
                        for k in range(3)
                    ]
                )
            for chunk in range(SLOTS // 8):
                sel = slice(8 * chunk, 8 * chunk + 8)
                total = [None] * 4 if opening else [acc[cell, chunk, k] for k in range(4)]
                for block, coords in zip(expo, far):
                    w = jnp.exp2(block[sel])
                    terms = [w, w * coords[0], w * coords[1], w * coords[2]]
                    total = [t if old is None else old + t for old, t in zip(total, terms)]
                if closing:
                    column = columns[sel]
                    for k in range(4):
                        summed = jnp.sum(total[k], axis=1, keepdims=True)
                        column = jnp.where(lane8 == cell * 4 + k, summed, column)
                    columns[sel] = column
                else:
                    for k in range(4):
                        acc[cell, chunk, k] = total[k]

    window = [(dy, dz) for dy in range(3) for dz in range(3)]
    phases = [
        [(0, dy, dz) for dy, dz in window[:8]],
        [(0, 2, 2)] + [(1, dy, dz) for dy, dz in window],
        [(2, dy, dz) for dy, dz in window],
    ]

    def sweep(phase):
        @pl.loop(0, CELLS // UNROLL)
        def _(step):
            for part in range(UNROLL):
                pairs(step * UNROLL + part, phases[phase], phase == 0, phase == 2)

    put_mask(0, mask_own[...])

    def turn_body(turn, carry):
        q = qs[turn]
        frame = [q[0:16] - 0.5, q[16:32] + off_y, q[32:48] + off_z]
        put_own(frame)
        put_far(0, q, -0.5)
        sweep(0)

        @pl.when(turn == 0)
        def _():
            for side in range(2):
                mask_copy(side).wait()
            for slot in range(2):
                put_mask(1 + slot, mask_halo[order[slot]])

        for slot in range(2):
            side = order[slot]
            slab_landing(turn, side).wait_recv()
            put_far(1 + slot, halo[turn, side], jnp.where(side == 0, 0.5, -1.5))
            sweep(1 + slot)

        sums[...] = columns[...].T
        for side in range(2):
            slab_copy(turn, side).wait_send()
            bead_copy(turn, side).wait()
        before, behind = chain[turn, 1], chain[turn, 0]
        spring = -SPRING * ((2.0 * q - before) - behind)
        here = jnp.where(mask_own[...] == 0.0, PAIR_SCALE, 0.0)
        total = [sums[pl.ds(k, CELLS, stride=4), :] for k in range(4)]
        finish = jnp.where(turn > 0, HALF_STEP, 0.0)
        begin = jnp.where(turn < STEPS, HALF_STEP, 0.0)
        after = jnp.minimum(turn + 1, STEPS)
        advance = jnp.where(turn < STEPS, TIME_STEP, 0.0)
        for k in range(3):
            sel = slice(16 * k, 16 * k + 16)
            force = (frame[k] * total[0] - total[1 + k]) * here + spring[sel]
            v = vel_out[sel] + finish * force
            v = v + begin * force
            vel_out[sel] = v
            pos_out[sel] = q[sel] + advance * v

        @pl.when(turn < STEPS)
        def _():
            qs[turn + 1] = pos_out[...]
            send(turn + 1)

        return carry

    lax.fori_loop(0, EVALS, turn_body, 0)


def local(positions, velocities, counts):
    rows = 3 * CELLS
    beads, slabs = lax.axis_size("bead"), lax.axis_size("slab")
    f32, bf16 = jnp.float32, jnp.bfloat16
    vmem = pl.BlockSpec(memory_space=pltpu.VMEM)
    out = pl.pallas_call(
        functools.partial(kernel, beads, slabs),
        out_shape=[jax.ShapeDtypeStruct((rows, SLOTS), f32)] * 2,
        in_specs=[vmem, vmem, pl.BlockSpec(memory_space=pltpu.SMEM)],
        out_specs=[vmem, vmem],
        scratch_shapes=[
            pltpu.VMEM((EVALS, rows, SLOTS), f32),
            pltpu.VMEM((EVALS, 2, rows, SLOTS), f32),
            pltpu.VMEM((EVALS, 2, rows, SLOTS), f32),
            pltpu.VMEM((CELLS, SLOTS), f32),
            pltpu.VMEM((2, CELLS, SLOTS), f32),
            pltpu.VMEM((3, 6, 8, SLOTS), f32),
            pltpu.VMEM((CELLS * OWN_STRIDE, SLOTS), f32),
            pltpu.VMEM((3 * 48 * FAR_STRIDE + 8, SLOTS), f32),
            pltpu.VMEM((CELLS, SLOTS, FEATS), bf16),
            pltpu.VMEM((3, 6, FEATS, 6 * SLOTS), bf16),
            pltpu.VMEM((3, 3, 6, 8, SLOTS), f32),
            pltpu.VMEM((CELLS, SLOTS // 8, 4, 8, SLOTS), f32),
            pltpu.VMEM((SLOTS, SLOTS), f32),
            pltpu.VMEM((SLOTS, SLOTS), f32),
            pltpu.VMEM((SLOTS, SLOTS), bf16),
            pltpu.SemaphoreType.DMA((EVALS, 4)),
            pltpu.SemaphoreType.DMA((EVALS, 4)),
            pltpu.SemaphoreType.DMA((2,)),
            pltpu.SemaphoreType.DMA((2,)),
        ],
        compiler_params=pltpu.CompilerParams(collective_id=0, has_side_effects=True),
        name="verlet",
    )(positions.reshape(rows, SLOTS), velocities.reshape(rows, SLOTS), counts)
    return tuple(o.reshape(positions.shape) for o in out)


def solution(mesh):
    spec = P("bead", None, "slab", None, None, None)
    return jax.shard_map(
        local,
        mesh=mesh,
        in_specs=(spec, spec, P("slab", None, None)),
        out_specs=(spec, spec),
        check_vma=False,
    )
```

```python
import functools

import jax
import jax.numpy as jnp
from jax import lax
from jax.experimental import pallas as pl
from jax.experimental.pallas import tpu as pltpu
from jax.sharding import PartitionSpec as P

STEPS = 4
EVALS = STEPS + 1

PAIR_SCALE = 0.08
WIDTH_FACTOR = 2.0
SPRING = 4.0
HALF_STEP = 0.025
TIME_STEP = 0.05

LOG2E = 1.4426950408889634
ALPHA = WIDTH_FACTOR * LOG2E
ABSENT = -1e30

CELLS = 16
SLOTS = 128
FEATS = 32
OWN_STRIDE, FAR_STRIDE = 33, 25
UNROLL = 16
STRIDE = 8
MESH = pl.DeviceIdType.MESH


def split3(value):
    high = value.astype(jnp.bfloat16).astype(jnp.float32)
    rest = value - high
    mid = rest.astype(jnp.bfloat16).astype(jnp.float32)
    return high, mid, rest - mid


def far_rows(coords):
    rows = []
    for coord in coords:
        h, m, l = split3(coord)
        rows += [h, m, l, h, m, h]
    norm = -ALPHA * (coords[0] * coords[0] + coords[1] * coords[1] + coords[2] * coords[2])
    return rows + list(split3(norm))


def own_rows(coords):
    rows = []
    for coord in coords:
        h, m, l = split3((2.0 * ALPHA) * coord)
        rows += [h, h, h, m, m, l]
    norm = -ALPHA * (coords[0] * coords[0] + coords[1] * coords[1] + coords[2] * coords[2])
    return list(enumerate(rows)) + list(enumerate(split3(norm), 21))


def kernel(
    beads, slabs,
    pos_in, vel_in, counts, out,
    qs, vel, halo, chain, mask_own, mask_halo, ext, own32, far32, own_feats, far_feats, far_coords,
    acc, columns, sums, eye,
    send_sem, recv_sem, mask_send, mask_recv, load_sem,
):
    bead, slab = lax.axis_index("bead"), lax.axis_index("slab")
    slab_up, slab_down = lax.rem(slab + 1, slabs), lax.rem(slab + slabs - 1, slabs)
    bead_up, bead_down = lax.rem(bead + 1, beads), lax.rem(bead + beads - 1, beads)
    partners = [(bead, slab_up), (bead, slab_down), (bead_up, slab), (bead_down, slab)]
    near = jnp.where(lax.rem(slab, 4) == 3, 1, 0)
    order = [near, 1 - near]

    barrier = pltpu.get_barrier_semaphore()
    for partner in partners:
        pl.semaphore_signal(barrier, inc=1, device_id=partner, device_id_type=MESH)

    load_pos = pltpu.make_async_copy(pos_in, qs.at[0], load_sem.at[0])
    load_vel = pltpu.make_async_copy(vel_in, vel, load_sem.at[1])
    load_pos.start()
    load_vel.start()

    lanes = lax.broadcasted_iota(jnp.int32, (1, SLOTS), 1)
    for cell in range(CELLS):
        here = lanes < counts[0, cell // 4, cell % 4]
        mask_own[cell : cell + 1, :] = jnp.where(here, 0.0, ABSENT)
    load_pos.wait()
    pl.semaphore_wait(barrier, 4)

    def mask_copy(side):
        return pltpu.make_async_remote_copy(
            src_ref=mask_own,
            dst_ref=mask_halo.at[1 - side],
            send_sem=mask_send.at[side],
            recv_sem=mask_recv.at[1 - side],
            device_id=partners[side],
            device_id_type=MESH,
        )

    def slab_copy(turn, side):
        return pltpu.make_async_remote_copy(
            src_ref=qs.at[turn],
            dst_ref=halo.at[turn, 1 - side],
            send_sem=send_sem.at[turn, side],
            recv_sem=recv_sem.at[turn, 1 - side],
            device_id=partners[side],
            device_id_type=MESH,
        )

    def slab_landing(turn, side):
        return pltpu.make_async_remote_copy(
            src_ref=qs.at[turn],
            dst_ref=halo.at[turn, side],
            send_sem=send_sem.at[turn, 0],
            recv_sem=recv_sem.at[turn, side],
            device_id=partners[0],
            device_id_type=MESH,
        )

    def bead_copy(turn, side):
        return pltpu.make_async_remote_copy(
            src_ref=qs.at[turn],
            dst_ref=chain.at[turn, 1 - side],
            send_sem=send_sem.at[turn, 2 + side],
            recv_sem=recv_sem.at[turn, 3 - side],
            device_id=partners[2 + side],
            device_id_type=MESH,
        )

    def send(turn):
        for side in range(2):
            slab_copy(turn, side).start()
        for side in range(2):
            bead_copy(turn, side).start()

    for side in range(2):
        mask_copy(side).start()
    send(0)

    one = jnp.ones((8, SLOTS), jnp.float32)
    zero = jnp.zeros((8, SLOTS), jnp.float32)
    for group in range(2):
        for row in range(FEATS):
            if row in (18, 19, 20) or row >= 24:
                at = pl.ds(group * 8 * OWN_STRIDE + row, 8, stride=OWN_STRIDE)
                own32[at, :] = one if row <= 24 else zero
    for group in range(18):
        for row in (21, 22, 23):
            far32[pl.ds(group * 8 * FAR_STRIDE + row, 8, stride=FAR_STRIDE), :] = one
    far32[3 * 48 * FAR_STRIDE :, :] = zero
    ext[...] = jnp.zeros_like(ext)
    columns[...] = jnp.zeros_like(columns)
    row_id = lax.broadcasted_iota(jnp.int32, (SLOTS, SLOTS), 0)
    lane_id = lax.broadcasted_iota(jnp.int32, (SLOTS, SLOTS), 1)
    eye[...] = jnp.where(row_id == lane_id, 1.0, 0.0).astype(jnp.bfloat16)

    cell_id = lax.broadcasted_iota(jnp.int32, (CELLS, SLOTS), 0)
    off_y = (cell_id // 4).astype(jnp.float32) - 2.0
    off_z = (cell_id % 4).astype(jnp.float32) - 2.0
    zz_off = lax.broadcasted_iota(jnp.int32, (8, SLOTS), 0).astype(jnp.float32) - 3.0
    lane8 = lax.broadcasted_iota(jnp.int32, (8, SLOTS), 1)

    def extend(comp, rows):
        for yy in range(6):
            y = (yy + 3) % 4
            ext[comp, yy, 1:5, :] = rows[4 * y : 4 * y + 4]
            ext[comp, yy, 0:1, :] = rows[4 * y + 3 : 4 * y + 4]
            ext[comp, yy, 5:6, :] = rows[4 * y : 4 * y + 1]

    def put_mask(slot, mask):
        extend(0, mask)
        for yy in range(6):
            far32[pl.ds((slot * 48 + yy * 8) * FAR_STRIDE + 24, 8, stride=FAR_STRIDE), :] = ext[0, yy]

    def put_far(slot, q, shift):
        for comp in range(3):
            extend(comp, q[16 * comp : 16 * comp + 16])
        for yy in range(6):
            coords = [ext[0, yy] + shift, ext[1, yy] + (yy - 3.0), ext[2, yy] + zz_off]
            for comp in range(3):
                far_coords[slot, comp, yy] = coords[comp]
            base = (slot * 48 + yy * 8) * FAR_STRIDE
            for k, row in enumerate(far_rows(coords)):
                far32[pl.ds(base + k, 8, stride=FAR_STRIDE), :] = row
        for yy in range(6):
            for zz in range(6):
                at = (slot * 48 + yy * 8 + zz) * FAR_STRIDE
                far_feats[slot, yy, :, zz * SLOTS : (zz + 1) * SLOTS] = far32[
                    at : at + FEATS, :
                ].astype(jnp.bfloat16)

    def put_own(coords):
        for half in range(2):
            sel = slice(8 * half, 8 * half + 8)
            for k, row in own_rows([coord[sel] for coord in coords]):
                own32[pl.ds(8 * half * OWN_STRIDE + k, 8, stride=OWN_STRIDE), :] = row
        for cell in range(CELLS):
            block = own32[cell * OWN_STRIDE : cell * OWN_STRIDE + FEATS, :].astype(jnp.bfloat16)
            turned = lax.dot_general(
                eye[...], block, (((1,), (1,)), ((), ())), preferred_element_type=jnp.float32
            )
            own_feats[cell] = turned.astype(jnp.bfloat16)

    def pairs(cell, blocks, first, last):
        cy, cz = cell // 4, lax.rem(cell, 4)
        feats = own_feats[cell]
        for start in range(0, len(blocks), STRIDE):
            group = blocks[start : start + STRIDE]
            opening, closing = first and start == 0, last and start + STRIDE >= len(blocks)
            expo, far = [], []
            for tile in range(0, len(group), 2):
                sides = [
                    far_feats[slot, cy + dy, :, pl.ds(pl.multiple_of((cz + dz) * SLOTS, SLOTS), SLOTS)]
                    for slot, dy, dz in group[tile : tile + 2]
                ]
                side = sides[0] if len(sides) == 1 else jnp.concatenate(sides, axis=1)
                both = jnp.dot(feats, side, preferred_element_type=jnp.float32)
                expo += [both[:, n * SLOTS : (n + 1) * SLOTS] for n in range(len(sides))]
            for slot, dy, dz in group:
                far.append(
                    [
                        jnp.broadcast_to(
                            far_coords[slot, k, cy + dy, pl.ds(cz + dz, 1), :], (8, SLOTS)
                        )
                        for k in range(3)
                    ]
                )
            for chunk in range(SLOTS // 8):
                sel = slice(8 * chunk, 8 * chunk + 8)
                total = [None] * 4 if opening else [acc[cell, chunk, k] for k in range(4)]
                for block, coords in zip(expo, far):
                    w = jnp.exp2(block[sel])
                    terms = [w, w * coords[0], w * coords[1], w * coords[2]]
                    total = [t if old is None else old + t for old, t in zip(total, terms)]
                if closing:
                    column = columns[sel]
                    for k in range(4):
                        summed = jnp.sum(total[k], axis=1, keepdims=True)
                        column = jnp.where(lane8 == cell * 4 + k, summed, column)
                    columns[sel] = column
                else:
                    for k in range(4):
                        acc[cell, chunk, k] = total[k]

    window = [(dy, dz) for dy in range(3) for dz in range(3)]
    phases = [
        [(0, dy, dz) for dy, dz in window[:8]],
        [(0, 2, 2)] + [(1, dy, dz) for dy, dz in window],
        [(2, dy, dz) for dy, dz in window],
    ]

    def sweep(phase):
        @pl.loop(0, CELLS // UNROLL)
        def _(step):
            for part in range(UNROLL):
                pairs(step * UNROLL + part, phases[phase], phase == 0, phase == 2)

    put_mask(0, mask_own[...])

    def turn_body(turn, carry):
        q = qs[turn]
        frame = [q[0:16] - 0.5, q[16:32] + off_y, q[32:48] + off_z]
        put_own(frame)
        put_far(0, q, -0.5)
        sweep(0)

        @pl.when(turn == 0)
        def _():
            load_vel.wait()
            for side in range(2):
                mask_copy(side).wait()
            for slot in range(2):
                put_mask(1 + slot, mask_halo[order[slot]])

        for slot in range(2):
            side = order[slot]
            slab_landing(turn, side).wait_recv()
            put_far(1 + slot, halo[turn, side], jnp.where(side == 0, 0.5, -1.5))
            sweep(1 + slot)

        sums[...] = columns[...].T
        for side in range(2):
            slab_copy(turn, side).wait_send()
            bead_copy(turn, side).wait()
        before, behind = chain[turn, 1], chain[turn, 0]
        spring = -SPRING * ((2.0 * q - before) - behind)
        here = jnp.where(mask_own[...] == 0.0, PAIR_SCALE, 0.0)
        total = [sums[pl.ds(k, CELLS, stride=4), :] for k in range(4)]
        finish = jnp.where(turn > 0, HALF_STEP, 0.0)
        begin = jnp.where(turn < STEPS, HALF_STEP, 0.0)
        after = jnp.minimum(turn + 1, STEPS)
        advance = jnp.where(turn < STEPS, TIME_STEP, 0.0)
        for k in range(3):
            sel = slice(16 * k, 16 * k + 16)
            force = (frame[k] * total[0] - total[1 + k]) * here + spring[sel]
            v = vel[sel] + finish * force
            v = v + begin * force
            vel[sel] = v
            qs[turn + 1, sel] = q[sel] + advance * v

        @pl.when(turn < STEPS)
        def _():
            send(turn + 1)

        return carry

    lax.fori_loop(0, EVALS, turn_body, 0)
    out[0] = qs[EVALS]
    out[1] = vel[...]


def local(positions, velocities, counts):
    rows = 3 * CELLS
    beads, slabs = lax.axis_size("bead"), lax.axis_size("slab")
    f32, bf16 = jnp.float32, jnp.bfloat16
    vmem = pl.BlockSpec(memory_space=pltpu.VMEM)
    out = pl.pallas_call(
        functools.partial(kernel, beads, slabs),
        out_shape=jax.ShapeDtypeStruct((2, rows, SLOTS), f32),
        in_specs=[pl.BlockSpec(memory_space=pl.ANY)] * 2 + [pl.BlockSpec(memory_space=pltpu.SMEM)],
        out_specs=vmem,
        scratch_shapes=[
            pltpu.VMEM((EVALS + 1, rows, SLOTS), f32),
            pltpu.VMEM((rows, SLOTS), f32),
            pltpu.VMEM((EVALS, 2, rows, SLOTS), f32),
            pltpu.VMEM((EVALS, 2, rows, SLOTS), f32),
            pltpu.VMEM((CELLS, SLOTS), f32),
            pltpu.VMEM((2, CELLS, SLOTS), f32),
            pltpu.VMEM((3, 6, 8, SLOTS), f32),
            pltpu.VMEM((CELLS * OWN_STRIDE, SLOTS), f32),
            pltpu.VMEM((3 * 48 * FAR_STRIDE + 8, SLOTS), f32),
            pltpu.VMEM((CELLS, SLOTS, FEATS), bf16),
            pltpu.VMEM((3, 6, FEATS, 6 * SLOTS), bf16),
            pltpu.VMEM((3, 3, 6, 8, SLOTS), f32),
            pltpu.VMEM((CELLS, SLOTS // 8, 4, 8, SLOTS), f32),
            pltpu.VMEM((SLOTS, SLOTS), f32),
            pltpu.VMEM((SLOTS, SLOTS), f32),
            pltpu.VMEM((SLOTS, SLOTS), bf16),
            pltpu.SemaphoreType.DMA((EVALS, 4)),
            pltpu.SemaphoreType.DMA((EVALS, 4)),
            pltpu.SemaphoreType.DMA((2,)),
            pltpu.SemaphoreType.DMA((2,)),
            pltpu.SemaphoreType.DMA((2,)),
        ],
        compiler_params=pltpu.CompilerParams(collective_id=0, has_side_effects=True),
        name="verlet",
    )(positions.reshape(rows, SLOTS), velocities.reshape(rows, SLOTS), counts)
    return tuple(out[n].reshape(positions.shape) for n in range(2))


def solution(mesh):
    spec = P("bead", None, "slab", None, None, None)
    return jax.shard_map(
        local,
        mesh=mesh,
        in_specs=(spec, spec, P("slab", None, None)),
        out_specs=(spec, spec),
        check_vma=False,
    )
```

```python
import functools

import jax
import jax.numpy as jnp
from jax import lax
from jax.experimental import pallas as pl
from jax.experimental.pallas import tpu as pltpu
from jax.sharding import PartitionSpec as P

STEPS = 4
EVALS = STEPS + 1

PAIR_SCALE = 0.08
WIDTH_FACTOR = 2.0
SPRING = 4.0
HALF_STEP = 0.025
TIME_STEP = 0.05

LOG2E = 1.4426950408889634
ALPHA = WIDTH_FACTOR * LOG2E
ABSENT = -1e30

CELLS = 16
SLOTS = 128
FEATS = 32
OWN_STRIDE, FAR_STRIDE = 33, 25
UNROLL = 16
STRIDE = 8
MESH = pl.DeviceIdType.MESH


def split3(value):
    high = value.astype(jnp.bfloat16).astype(jnp.float32)
    rest = value - high
    mid = rest.astype(jnp.bfloat16).astype(jnp.float32)
    return high, mid, rest - mid


def far_rows(coords):
    rows = []
    for coord in coords:
        h, m, l = split3(coord)
        rows += [h, m, l, h, m, h]
    norm = -ALPHA * (coords[0] * coords[0] + coords[1] * coords[1] + coords[2] * coords[2])
    return rows + list(split3(norm))


def own_rows(coords):
    rows = []
    for coord in coords:
        h, m, l = split3((2.0 * ALPHA) * coord)
        rows += [h, h, h, m, m, l]
    norm = -ALPHA * (coords[0] * coords[0] + coords[1] * coords[1] + coords[2] * coords[2])
    return list(enumerate(rows)) + list(enumerate(split3(norm), 21))


def kernel(
    beads, slabs,
    pos_in, vel_in, counts, out,
    qs, vel, halo, chain, mask_own, mask_halo, ext, own32, far32, own_feats, far_feats, far_coords,
    acc, columns, sums,
    send_sem, recv_sem, mask_send, mask_recv, load_sem,
):
    bead, slab = lax.axis_index("bead"), lax.axis_index("slab")
    slab_up, slab_down = lax.rem(slab + 1, slabs), lax.rem(slab + slabs - 1, slabs)
    bead_up, bead_down = lax.rem(bead + 1, beads), lax.rem(bead + beads - 1, beads)
    partners = [(bead, slab_up), (bead, slab_down), (bead_up, slab), (bead_down, slab)]
    near = jnp.where(lax.rem(slab, 4) == 3, 1, 0)
    order = [near, 1 - near]

    barrier = pltpu.get_barrier_semaphore()
    for partner in partners:
        pl.semaphore_signal(barrier, inc=1, device_id=partner, device_id_type=MESH)

    load_pos = pltpu.make_async_copy(pos_in, qs.at[0], load_sem.at[0])
    load_vel = pltpu.make_async_copy(vel_in, vel, load_sem.at[1])
    load_pos.start()
    load_vel.start()

    lanes = lax.broadcasted_iota(jnp.int32, (1, SLOTS), 1)
    for cell in range(CELLS):
        here = lanes < counts[0, cell // 4, cell % 4]
        mask_own[cell : cell + 1, :] = jnp.where(here, 0.0, ABSENT)
    load_pos.wait()
    pl.semaphore_wait(barrier, 4)

    def mask_copy(side):
        return pltpu.make_async_remote_copy(
            src_ref=mask_own,
            dst_ref=mask_halo.at[1 - side],
            send_sem=mask_send.at[side],
            recv_sem=mask_recv.at[1 - side],
            device_id=partners[side],
            device_id_type=MESH,
        )

    def slab_copy(turn, side):
        return pltpu.make_async_remote_copy(
            src_ref=qs.at[turn],
            dst_ref=halo.at[turn, 1 - side],
            send_sem=send_sem.at[turn, side],
            recv_sem=recv_sem.at[turn, 1 - side],
            device_id=partners[side],
            device_id_type=MESH,
        )

    def slab_landing(turn, side):
        return pltpu.make_async_remote_copy(
            src_ref=qs.at[turn],
            dst_ref=halo.at[turn, side],
            send_sem=send_sem.at[turn, 0],
            recv_sem=recv_sem.at[turn, side],
            device_id=partners[0],
            device_id_type=MESH,
        )

    def bead_copy(turn, side):
        return pltpu.make_async_remote_copy(
            src_ref=qs.at[turn],
            dst_ref=chain.at[turn, 1 - side],
            send_sem=send_sem.at[turn, 2 + side],
            recv_sem=recv_sem.at[turn, 3 - side],
            device_id=partners[2 + side],
            device_id_type=MESH,
        )

    def send(turn):
        for side in range(2):
            slab_copy(turn, side).start()
        for side in range(2):
            bead_copy(turn, side).start()

    for side in range(2):
        mask_copy(side).start()
    send(0)

    one = jnp.ones((8, SLOTS), jnp.float32)
    zero = jnp.zeros((8, SLOTS), jnp.float32)
    for group in range(2):
        for row in range(FEATS):
            if row in (18, 19, 20) or row >= 24:
                at = pl.ds(group * 8 * OWN_STRIDE + row, 8, stride=OWN_STRIDE)
                own32[at, :] = one if row <= 24 else zero
    for group in range(18):
        for row in (21, 22, 23):
            far32[pl.ds(group * 8 * FAR_STRIDE + row, 8, stride=FAR_STRIDE), :] = one
    far32[3 * 48 * FAR_STRIDE :, :] = zero
    ext[...] = jnp.zeros_like(ext)
    columns[...] = jnp.zeros_like(columns)
    cell_id = lax.broadcasted_iota(jnp.int32, (CELLS, SLOTS), 0)
    off_y = (cell_id // 4).astype(jnp.float32) - 2.0
    off_z = (cell_id % 4).astype(jnp.float32) - 2.0
    zz_off = lax.broadcasted_iota(jnp.int32, (8, SLOTS), 0).astype(jnp.float32) - 3.0
    lane8 = lax.broadcasted_iota(jnp.int32, (8, SLOTS), 1)

    def extend(comp, rows):
        for yy in range(6):
            y = (yy + 3) % 4
            ext[comp, yy, 1:5, :] = rows[4 * y : 4 * y + 4]
            ext[comp, yy, 0:1, :] = rows[4 * y + 3 : 4 * y + 4]
            ext[comp, yy, 5:6, :] = rows[4 * y : 4 * y + 1]

    def put_mask(slot, mask):
        extend(0, mask)
        for yy in range(6):
            far32[pl.ds((slot * 48 + yy * 8) * FAR_STRIDE + 24, 8, stride=FAR_STRIDE), :] = ext[0, yy]

    def put_far(slot, q, shift):
        for comp in range(3):
            extend(comp, q[16 * comp : 16 * comp + 16])
        for yy in range(6):
            coords = [ext[0, yy] + shift, ext[1, yy] + (yy - 3.0), ext[2, yy] + zz_off]
            for comp in range(3):
                far_coords[slot, comp, yy] = coords[comp]
            base = (slot * 48 + yy * 8) * FAR_STRIDE
            for k, row in enumerate(far_rows(coords)):
                far32[pl.ds(base + k, 8, stride=FAR_STRIDE), :] = row
        for yy in range(6):
            for zz in range(6):
                at = (slot * 48 + yy * 8 + zz) * FAR_STRIDE
                far_feats[slot, yy, :, zz * SLOTS : (zz + 1) * SLOTS] = far32[
                    at : at + FEATS, :
                ].astype(jnp.bfloat16)

    def put_own(coords):
        for half in range(2):
            sel = slice(8 * half, 8 * half + 8)
            for k, row in own_rows([coord[sel] for coord in coords]):
                own32[pl.ds(8 * half * OWN_STRIDE + k, 8, stride=OWN_STRIDE), :] = row
        for cell in range(CELLS):
            block = own32[cell * OWN_STRIDE : cell * OWN_STRIDE + FEATS, :]
            own_feats[cell] = block.T.astype(jnp.bfloat16)

    def pairs(cell, blocks, first, last):
        cy, cz = cell // 4, lax.rem(cell, 4)
        feats = own_feats[cell]
        for start in range(0, len(blocks), STRIDE):
            group = blocks[start : start + STRIDE]
            opening, closing = first and start == 0, last and start + STRIDE >= len(blocks)
            expo, far = [], []
            for tile in range(0, len(group), 2):
                sides = [
                    far_feats[slot, cy + dy, :, pl.ds(pl.multiple_of((cz + dz) * SLOTS, SLOTS), SLOTS)]
                    for slot, dy, dz in group[tile : tile + 2]
                ]
                side = sides[0] if len(sides) == 1 else jnp.concatenate(sides, axis=1)
                both = jnp.dot(feats, side, preferred_element_type=jnp.float32)
                expo += [both[:, n * SLOTS : (n + 1) * SLOTS] for n in range(len(sides))]
            for slot, dy, dz in group:
                far.append(
                    [
                        jnp.broadcast_to(
                            far_coords[slot, k, cy + dy, pl.ds(cz + dz, 1), :], (8, SLOTS)
                        )
                        for k in range(3)
                    ]
                )
            for chunk in range(SLOTS // 8):
                sel = slice(8 * chunk, 8 * chunk + 8)
                total = [None] * 4 if opening else [acc[cell, chunk, k] for k in range(4)]
                for block, coords in zip(expo, far):
                    w = jnp.exp2(block[sel])
                    terms = [w, w * coords[0], w * coords[1], w * coords[2]]
                    total = [t if old is None else old + t for old, t in zip(total, terms)]
                if closing:
                    column = columns[sel]
                    for k in range(4):
                        summed = jnp.sum(total[k], axis=1, keepdims=True)
                        column = jnp.where(lane8 == cell * 4 + k, summed, column)
                    columns[sel] = column
                else:
                    for k in range(4):
                        acc[cell, chunk, k] = total[k]

    window = [(dy, dz) for dy in range(3) for dz in range(3)]
    phases = [
        [(0, dy, dz) for dy, dz in window[:8]],
        [(0, 2, 2)] + [(1, dy, dz) for dy, dz in window],
        [(2, dy, dz) for dy, dz in window],
    ]

    def sweep(phase):
        @pl.loop(0, CELLS // UNROLL)
        def _(step):
            for part in range(UNROLL):
                pairs(step * UNROLL + part, phases[phase], phase == 0, phase == 2)

    put_mask(0, mask_own[...])

    def turn_body(turn, carry):
        q = qs[turn]
        frame = [q[0:16] - 0.5, q[16:32] + off_y, q[32:48] + off_z]
        put_own(frame)
        put_far(0, q, -0.5)
        sweep(0)

        @pl.when(turn == 0)
        def _():
            load_vel.wait()
            for side in range(2):
                mask_copy(side).wait()
            for slot in range(2):
                put_mask(1 + slot, mask_halo[order[slot]])

        for slot in range(2):
            side = order[slot]
            slab_landing(turn, side).wait_recv()
            put_far(1 + slot, halo[turn, side], jnp.where(side == 0, 0.5, -1.5))
            sweep(1 + slot)

        sums[...] = columns[...].T
        for side in range(2):
            slab_copy(turn, side).wait_send()
            bead_copy(turn, side).wait()
        before, behind = chain[turn, 1], chain[turn, 0]
        spring = -SPRING * ((2.0 * q - before) - behind)
        here = jnp.where(mask_own[...] == 0.0, PAIR_SCALE, 0.0)
        total = [sums[pl.ds(k, CELLS, stride=4), :] for k in range(4)]
        finish = jnp.where(turn > 0, HALF_STEP, 0.0)
        begin = jnp.where(turn < STEPS, HALF_STEP, 0.0)
        after = jnp.minimum(turn + 1, STEPS)
        advance = jnp.where(turn < STEPS, TIME_STEP, 0.0)
        for k in range(3):
            sel = slice(16 * k, 16 * k + 16)
            force = (frame[k] * total[0] - total[1 + k]) * here + spring[sel]
            v = vel[sel] + finish * force
            v = v + begin * force
            vel[sel] = v
            qs[turn + 1, sel] = q[sel] + advance * v

        @pl.when(turn < STEPS)
        def _():
            send(turn + 1)

        return carry

    lax.fori_loop(0, EVALS, turn_body, 0)
    out[0] = qs[EVALS]
    out[1] = vel[...]


def local(positions, velocities, counts):
    rows = 3 * CELLS
    beads, slabs = lax.axis_size("bead"), lax.axis_size("slab")
    f32, bf16 = jnp.float32, jnp.bfloat16
    vmem = pl.BlockSpec(memory_space=pltpu.VMEM)
    out = pl.pallas_call(
        functools.partial(kernel, beads, slabs),
        out_shape=jax.ShapeDtypeStruct((2, rows, SLOTS), f32),
        in_specs=[pl.BlockSpec(memory_space=pl.ANY)] * 2 + [pl.BlockSpec(memory_space=pltpu.SMEM)],
        out_specs=vmem,
        scratch_shapes=[
            pltpu.VMEM((EVALS + 1, rows, SLOTS), f32),
            pltpu.VMEM((rows, SLOTS), f32),
            pltpu.VMEM((EVALS, 2, rows, SLOTS), f32),
            pltpu.VMEM((EVALS, 2, rows, SLOTS), f32),
            pltpu.VMEM((CELLS, SLOTS), f32),
            pltpu.VMEM((2, CELLS, SLOTS), f32),
            pltpu.VMEM((3, 6, 8, SLOTS), f32),
            pltpu.VMEM((CELLS * OWN_STRIDE, SLOTS), f32),
            pltpu.VMEM((3 * 48 * FAR_STRIDE + 8, SLOTS), f32),
            pltpu.VMEM((CELLS, SLOTS, FEATS), bf16),
            pltpu.VMEM((3, 6, FEATS, 6 * SLOTS), bf16),
            pltpu.VMEM((3, 3, 6, 8, SLOTS), f32),
            pltpu.VMEM((CELLS, SLOTS // 8, 4, 8, SLOTS), f32),
            pltpu.VMEM((SLOTS, SLOTS), f32),
            pltpu.VMEM((SLOTS, SLOTS), f32),
            pltpu.SemaphoreType.DMA((EVALS, 4)),
            pltpu.SemaphoreType.DMA((EVALS, 4)),
            pltpu.SemaphoreType.DMA((2,)),
            pltpu.SemaphoreType.DMA((2,)),
            pltpu.SemaphoreType.DMA((2,)),
        ],
        compiler_params=pltpu.CompilerParams(collective_id=0, has_side_effects=True),
        name="verlet",
    )(positions.reshape(rows, SLOTS), velocities.reshape(rows, SLOTS), counts)
    return tuple(out[n].reshape(positions.shape) for n in range(2))


def solution(mesh):
    spec = P("bead", None, "slab", None, None, None)
    return jax.shard_map(
        local,
        mesh=mesh,
        in_specs=(spec, spec, P("slab", None, None)),
        out_specs=(spec, spec),
        check_vma=False,
    )
```
